32 devices in a mesh: cuts: 1, mode: 32 (over z, y, x, core).
Axes of the slice: x: 2, y: 2, z: 4, core: 2. Of those that a mesh axis runs over, the one named last changes fastest.
Arguments:
- branch_in: bfloat16 [4, 2, 2048, 1024], P(None, None, ('cuts', 'mode')), may hold values from -6 to 6
- column_order: int32 [4, 1024], replicated, may hold values from 0 to 1023, each once within a row
- gate_a: bfloat16 [2, 1024, 1024], P(None, 'mode'), may hold values from -0.125 to 0.125
- gate_b: bfloat16 [2, 1024, 1024], P(None, 'mode'), may hold values from -0.125 to 0.125
Outputs:
- joined: bfloat16 [2, 512, 2, 128], P(None, ('cuts', 'mode'))
The draws below stay inside these ranges and needn't reach their ends.
Inputs may be any that keep to these rules, and one draw needn't show every extreme that they name: Each row of column_order names every column state once.
All inputs are finite; a program needn't handle non-finite values.
Results may differ from the reference program's by a relative error of at most 0.014.
Values may be sent and summed in bfloat16 or wider, within the bound.
A program may use at most 128 MiB of HBM per device.

```python
import jax
import jax.numpy as jnp

C = 1024
SHARED = 4096
RD = 64
KEPT = 4
CYCLES = 2
ROWS = 2048
GROUP = 32
JOIN = 128
N_MODE = 32


def level_of(rng, dims, cuts, smallest, high):
    factor_of = 1.0
    for position, shards_of in cuts:
        draws = jax.random.uniform(jax.random.fold_in(jax.random.fold_in(rng, 6), position), (shards_of,), jnp.float32, smallest / len(cuts), high / len(cuts))
        factor_of = factor_of * jnp.repeat(jnp.exp(draws), dims[position] // shards_of).reshape((-1,) + (1,) * (len(dims) - 1 - position))
    return factor_of


def normal_values(own_key, shape, scale, most, cuts=(), dtype=jnp.bfloat16):
    result = scale * jax.random.normal(own_key, shape, jnp.float32)
    if cuts:
        result = result * level_of(own_key, shape, cuts, -0.22, 0.18)
    return jnp.clip(result, -most, most).astype(dtype)


def setup_inputs(seed: int = 0, part: int = 0) -> dict:
    key_list = jax.random.split(jax.random.key(seed), 5)
    part_keys = jax.random.split(jax.random.fold_in(key_list[4], part), 5)
    return {
        "branch_in": normal_values(part_keys[0], (4, 2, ROWS, C), 1.0, 6.0, ((2, 32),)),
        "column_order": jax.vmap(lambda own: jax.random.permutation(own, C))(jax.random.split(key_list[1], 4)).reshape((4, C)).astype(jnp.int32),
        "gate_a": normal_values(key_list[2], (2, C, C), (2 * C) ** -0.5, 0.125, ((1, 32),)),
        "gate_b": normal_values(key_list[3], (2, C, C), (2 * C) ** -0.5, 0.125, ((1, 32),)),
    }


def complex_product(pair_tensor, layer_block):
    real_part = jnp.dot(pair_tensor[0], layer_block[0], preferred_element_type=jnp.float32) - jnp.dot(pair_tensor[1], layer_block[1], preferred_element_type=jnp.float32)
    imag_part = jnp.dot(pair_tensor[0], layer_block[1], preferred_element_type=jnp.float32) + jnp.dot(pair_tensor[1], layer_block[0], preferred_element_type=jnp.float32)
    return jnp.stack([real_part, imag_part]).astype(jnp.bfloat16)


def regroup(pair_tensor):
    pieces = pair_tensor.reshape(2, N_MODE, RD, N_MODE, GROUP)
    return jnp.transpose(pieces, (0, 3, 2, 1, 4)).reshape(2, ROWS, C)


def reference(branch_in, column_order, gate_a, gate_b):
    join_scale = (2.0 * SHARED) ** -0.5
    finals = []
    for branch in range(4):
        state = jnp.take(branch_in[branch], column_order[branch].astype(jnp.int32), axis=2)
        for layer_number in range(2 * CYCLES):
            if layer_number > 0:
                state = regroup(state)
            layer_block = gate_a if layer_number % 2 == 0 else gate_b
            state = complex_product(state, layer_block)
        finals.append(state)
    results = []
    for pair_number in range(2):
        left_part = finals[2 * pair_number].reshape(2, KEPT, JOIN, SHARED)
        right_part = finals[2 * pair_number + 1].reshape(2, SHARED, KEPT, JOIN)
        blocks = []
        for batch in range(KEPT):
            left_real = left_part[0, batch]
            left_imag = left_part[1, batch]
            right_real = right_part[0, :, batch, :]
            right_imag = right_part[1, :, batch, :]
            real_part = jnp.dot(left_real, right_real, preferred_element_type=jnp.float32) - jnp.dot(left_imag, right_imag, preferred_element_type=jnp.float32)
            imag_part = jnp.dot(left_real, right_imag, preferred_element_type=jnp.float32) + jnp.dot(left_imag, right_real, preferred_element_type=jnp.float32)
            blocks.append(jnp.stack([real_part, imag_part], axis=1))
        stacked = jnp.concatenate(blocks, axis=0)
        results.append((stacked * join_scale).astype(jnp.bfloat16))
    return jnp.stack(results)
```

```python
import jax
import jax.numpy as jnp
from jax import lax
from jax.sharding import PartitionSpec as P

SHARED = 4096
KEPT = 4
CYCLES = 2
F32 = jnp.float32
BF16 = jnp.bfloat16


def complex_dot(left_real, left_imag, right_real, right_imag):
    real_part = jnp.dot(left_real, right_real, preferred_element_type=F32) - jnp.dot(
        left_imag, right_imag, preferred_element_type=F32
    )
    imag_part = jnp.dot(left_real, right_imag, preferred_element_type=F32) + jnp.dot(
        left_imag, right_real, preferred_element_type=F32
    )
    return real_part, imag_part


def layers_plain(state, orders, whole_a, whole_b):
    parts, devices, sides, share, width = state.shape
    group = width // devices
    iota = lax.broadcasted_iota(jnp.int32, (width, width), 0)
    halves = []
    for side in range(sides):
        one_hot = (iota == orders[side][None, :]).astype(BF16)
        piece = state[:, :, side].reshape(parts * devices * share, width)
        halves.append(
            jnp.dot(piece, one_hot, preferred_element_type=F32)
            .astype(BF16)
            .reshape(parts, devices, share, width)
        )
    state = jnp.stack(halves, axis=2)
    for layer in range(2 * CYCLES):
        if layer > 0:
            pieces = state.reshape(parts, devices, sides, share, devices, group)
            state = pieces.transpose(0, 4, 2, 3, 1, 5)
        flat = state.reshape(parts, devices * sides * share, width)
        gate = whole_a if layer % 2 == 0 else whole_b
        state = jnp.stack(complex_dot(flat[0], flat[1], gate[0], gate[1])).astype(BF16)
    return state.reshape(parts, devices, sides, share, width)


def local(branch_in, column_order, gate_a, gate_b):
    join_scale = (2.0 * SHARED) ** (-0.5)
    devices = lax.axis_size("mode")
    me = lax.axis_index("mode")
    branches, parts, rows, width = branch_in.shape
    quarter = SHARED // width
    holders = devices // (2 * quarter)
    share = rows // (quarter * holders)
    pair = me // (quarter * holders)
    whole_a = lax.all_gather(gate_a, "mode", axis=1, tiled=True)
    whole_b = lax.all_gather(gate_b, "mode", axis=1, tiled=True)
    dealt = branch_in.reshape(2, 2, parts, holders, share, quarter, width)
    dealt = dealt.transpose(0, 5, 3, 2, 1, 4, 6).reshape(devices, parts, 2, share, width)
    dealt = lax.all_to_all(dealt, "mode", split_axis=0, concat_axis=0, tiled=True)
    state = dealt.transpose(1, 0, 2, 3, 4)
    orders = lax.dynamic_slice_in_dim(column_order, 2 * pair, 2, 0)
    state = layers_plain(state, orders, whole_a, whole_b)

    split = holders // KEPT
    piece = width // split
    free = devices * rows * width // (SHARED * KEPT)
    own_group = [
        [start * holders + h for h in range(holders)] for start in range(2 * quarter)
    ]
    pair_group = [
        [start * quarter * holders + d for d in range(quarter * holders)] for start in range(2)
    ]
    left = state[:, :, 0].reshape(parts, KEPT, devices // KEPT, share, split, piece)
    left = left.transpose(1, 4, 0, 2, 3, 5).reshape(
        holders, parts, devices // KEPT, share, piece
    )
    left = lax.all_to_all(
        left, "mode", split_axis=0, concat_axis=0, tiled=True, axis_index_groups=own_group
    )
    left = left.transpose(1, 2, 0, 3, 4).reshape(parts, free, piece)
    right = state[:, :, 1].reshape(parts, quarter, split, devices // (quarter * split), share, width)
    line = rows * width
    step = KEPT * free
    if width % step == 0:
        several = width // step
        right = right.reshape(
            parts, quarter, split, devices // (quarter * split), share, several, KEPT, free
        )
        right = right.transpose(1, 6, 2, 0, 3, 4, 5, 7)
        right = right.reshape(
            quarter * KEPT * split, parts, devices // (quarter * split), share, several, free
        )
        right = lax.all_to_all(
            right, "mode", split_axis=0, concat_axis=0, tiled=True, axis_index_groups=pair_group
        )
        right = right.reshape(
            quarter, holders, parts, devices // (quarter * split), share, several, free
        )
        right = right.transpose(2, 3, 1, 4, 0, 5, 6).reshape(parts, piece, free)
    else:
        spans = step // width
        kept_row = KEPT // spans
        right = right.reshape(
            parts, quarter, split, devices // (quarter * split), share, kept_row, free
        )
        own_j = me // holders % quarter
        g_high = own_j % spans
        slots = jnp.zeros(
            (quarter, spans, kept_row, split, parts, devices // (quarter * split), share, free), BF16
        )
        filled = right.transpose(1, 5, 2, 0, 3, 4, 6)
        slots = lax.dynamic_update_slice_in_dim(slots, filled[:, None], g_high, 1)
        slots = slots.reshape(
            quarter * KEPT * split, parts, devices // (quarter * split), share, free
        )
        slots = lax.all_to_all(
            slots, "mode", split_axis=0, concat_axis=0, tiled=True, axis_index_groups=pair_group
        )
        slots = slots.reshape(
            quarter // spans, spans, holders, parts, devices // (quarter * split), share, free
        )
        my_g = me % holders // split
        slots = lax.dynamic_index_in_dim(slots, my_g // kept_row, 1, keepdims=False)
        right = slots.transpose(2, 3, 1, 4, 0, 5).reshape(parts, piece, free)
    real_part, imag_part = complex_dot(left[0], left[1], right[0], right[1])
    partial = jnp.stack([real_part, imag_part], axis=1)
    return finish(partial, join_scale, devices, quarter, split)


def finish(partial, join_scale, devices, quarter, split):
    me = lax.axis_index("mode")
    free = partial.shape[0]
    holders = devices // (2 * quarter)
    sum_group = [
        [((p * quarter + j) * KEPT + g) * split + w for j in range(quarter) for w in range(split)]
        for p in range(2)
        for g in range(KEPT)
    ]
    count = quarter * split
    chunks = partial.astype(BF16).reshape(count, free // count, 2, free)
    chunks = lax.all_to_all(
        chunks, "mode", split_axis=0, concat_axis=0, tiled=True, axis_index_groups=sum_group
    )
    done = (jnp.sum(chunks.astype(F32), axis=0) * join_scale).astype(BF16)
    halves = done.reshape(2, free // (2 * count), 2, free)
    pair = me // (quarter * holders)
    same = lax.dynamic_index_in_dim(halves, pair, 0, keepdims=False)
    other = lax.dynamic_index_in_dim(halves, 1 - pair, 0, keepdims=False)
    same_pairs, other_pairs = [], []
    for d in range(devices):
        p, j, g, w = (
            d // (quarter * holders),
            d // holders % quarter,
            d // split % KEPT,
            d % split,
        )
        base = g * (devices // KEPT) + 2 * (j * split + w)
        same_pairs.append((d, base + p))
        other_pairs.append((d, base + 1 - p))
    from_same = lax.ppermute(same, "mode", same_pairs)
    from_other = lax.ppermute(other, "mode", other_pairs)
    parity = me % 2
    first = jnp.where(parity == 0, from_same, from_other)
    second = jnp.where(parity == 0, from_other, from_same)
    return jnp.stack([first, second])


def solution(mesh):
    in_specs = (
        P(None, None, ("cuts", "mode"), None),
        P(),
        P(None, "mode", None),
        P(None, "mode", None),
    )
    out_specs = P(None, ("cuts", "mode"), None, None)
    return jax.shard_map(local, mesh=mesh, in_specs=in_specs, out_specs=out_specs, check_vma=False)
```

```python
import jax
import jax.numpy as jnp
from jax import lax
from jax.experimental import pallas as pl
from jax.experimental.pallas import tpu as pltpu
from jax.sharding import PartitionSpec as P

SHARED = 4096
KEPT = 4
CYCLES = 2
F32 = jnp.float32
BF16 = jnp.bfloat16


def complex_dot(left_real, left_imag, right_real, right_imag):
    real_part = jnp.dot(left_real, right_real, preferred_element_type=F32) - jnp.dot(
        left_imag, right_imag, preferred_element_type=F32
    )
    imag_part = jnp.dot(left_real, right_imag, preferred_element_type=F32) + jnp.dot(
        left_imag, right_real, preferred_element_type=F32
    )
    return real_part, imag_part


def layers_plain(state, orders, whole_a, whole_b):
    parts, devices, sides, share, width = state.shape
    group = width // devices
    iota = lax.broadcasted_iota(jnp.int32, (width, width), 0)
    halves = []
    for side in range(sides):
        one_hot = (iota == orders[side][None, :]).astype(BF16)
        piece = state[:, :, side].reshape(parts * devices * share, width)
        halves.append(
            jnp.dot(piece, one_hot, preferred_element_type=F32)
            .astype(BF16)
            .reshape(parts, devices, share, width)
        )
    state = jnp.stack(halves, axis=2)
    for layer in range(2 * CYCLES):
        if layer > 0:
            pieces = state.reshape(parts, devices, sides, share, devices, group)
            state = pieces.transpose(0, 4, 2, 3, 1, 5)
        flat = state.reshape(parts, devices * sides * share, width)
        gate = whole_a if layer % 2 == 0 else whole_b
        state = jnp.stack(complex_dot(flat[0], flat[1], gate[0], gate[1])).astype(BF16)
    return state.reshape(parts, devices, sides, share, width)


LANES = 128
HIGH = 8


def swap_lane_blocks(blocks, group):
    count = len(blocks)
    lane = lax.broadcasted_iota(jnp.int32, (HIGH, LANES), 1) // group
    bit = count // 2
    while bit:
        low = (lane // bit) % 2 == 0
        new = list(blocks)
        for i in range(count):
            if i & bit == 0:
                first, second = blocks[i], blocks[i | bit]
                new[i] = jnp.where(low, first, pltpu.roll(second, bit * group, 1))
                new[i | bit] = jnp.where(low, pltpu.roll(first, LANES - bit * group, 1), second)
        blocks = new
        bit //= 2
    return blocks


def whole_kernel(
    devices,
    dealt,
    orders,
    gate_a,
    gate_b,
    out,
    gates,
    landed,
    state,
    product,
    hot,
    mixer,
    left_out,
    right_out,
    left_in,
    right_in,
    part_out,
    part_in,
    own_sem,
    deal_send,
    deal_recv,
    gate_send,
    gate_recv,
    left_send,
    left_recv,
    right_send,
    right_recv,
    part_send,
    part_recv,
):
    me = lax.axis_index("mode")
    width = dealt.shape[2]
    rows = state.shape[1]
    groups = width // devices
    packed = LANES // groups
    holders = KEPT
    quarter = SHARED // width
    share = HIGH // 2
    barrier = pltpu.get_barrier_semaphore()

    def greet(o, carry):
        pl.semaphore_signal(barrier, inc=1, device_id={"mode": me ^ o})
        return carry

    lax.fori_loop(1, devices, greet, 0)

    def remote(src, dst, ssem, rsem, target):
        return pltpu.make_async_remote_copy(
            src_ref=src,
            dst_ref=dst,
            send_sem=ssem,
            recv_sem=rsem,
            device_id={"mode": target},
            device_id_type=pl.DeviceIdType.MESH,
        )

    z1, z0, y, x, c = (me // 16, me // 8 % 2, me // 4 % 2, me // 2 % 2, me % 2)
    every = slice(None)
    shards = (gate_a, gate_b)
    own = [
        pltpu.make_async_copy(shards[g], gates.at[g, :, z1, z0, y, x, c], own_sem.at[g])
        for g in range(2)
    ]
    own_x = pltpu.make_async_copy(dealt.at[me], landed.at[me], own_sem.at[2])
    for copy in own + [own_x]:
        copy.start()

    def region(g, part, index):
        return gates.at[(g, part) + index]

    steps = {
        "z0": (every, (z1, z0, y, x, c), 8),
        "z1": (every, (z1, every, y, x, c), 16),
        "p0": (0, (every, every, y, x, c), 4),
        "p1": (1, (every, every, y, x, c), 2),
        "q0": (0, (every, every, every, x, c), 2),
        "q1": (1, (every, every, y, every, c), 4),
        "c0": (every, (every, every, y, x, c), 1),
        "d0": (0, (every, every, 1 - y, x, c), 1),
        "d1": (1, (every, every, y, 1 - x, c), 1),
        "e0": (0, (every, every, every, 1 - x, c), 1),
        "e1": (1, (every, every, 1 - y, every, c), 1),
    }
    names = list(steps)

    def gate_copy(g, name):
        part, index, bit = steps[name]
        k = names.index(name)
        here = region(g, part, index)
        src = shards[g] if name == "z0" else here
        return remote(src, here, gate_send.at[g, k], gate_recv.at[g, k], me ^ bit)

    def send(g, *which):
        for name in which:
            gate_copy(g, name).start()

    def arrive(g, *which):
        for name in which:
            gate_copy(g, name).wait_recv()

    def deal_copy(o):
        return remote(dealt.at[me ^ o], landed.at[me], deal_send.at[o], deal_recv.at[o], me ^ o)

    def start_deal(o, carry):
        deal_copy(o).start()
        return carry

    pl.semaphore_wait(barrier, devices - 1)
    send(0, "z0")
    send(1, "z0")
    lax.fori_loop(1, 8, start_deal, 0)
    k = lax.broadcasted_iota(jnp.int32, (width, width), 1)
    natural = (
        (k % 32 // share) * 128 + (k // 64 % 4) * 32 + (k % share) * 8 + (k // 256) * 2 + k // 32 % 2
    )
    for copy in own:
        copy.wait()
    arrive(0, "z0")
    send(0, "z1")
    arrive(1, "z0")
    send(1, "z1")
    lax.fori_loop(8, devices, start_deal, 0)
    mixer[...] = jnp.where(
        lax.broadcasted_iota(jnp.int32, (width, width), 0) == natural, 1.0, 0.0
    ).astype(BF16)
    arrive(0, "z1")
    send(0, "p0", "p1", "c0")
    arrive(1, "z1")
    send(1, "p0", "p1", "c0")
    arrive(0, "p0", "p1")
    send(0, "q0", "q1", "d0", "d1")
    arrive(1, "p0", "p1")
    send(1, "q0", "q1", "d0", "d1")

    own_x.wait()

    def wait_deal(o, carry):
        remote(dealt.at[me], landed.at[me ^ o], deal_send.at[o], deal_recv.at[o], me ^ o).wait_recv()
        return carry

    lax.fori_loop(1, devices, wait_deal, 0)
    wide = landed[...].astype(F32)
    for part in range(2):
        state[part] = wide[:, part * HIGH : (part + 1) * HIGH].reshape(rows, width).astype(BF16)
    first_side = lax.broadcasted_iota(jnp.int32, (rows, width // 4), 0) % HIGH < share
    for side in range(2):
        source = lax.broadcasted_iota(jnp.int32, (width, width), 0)
        hot[side] = jnp.where(source == orders[side : side + 1, :], 1.0, 0.0).astype(BF16)

    def tile_of(n):
        return pl.ds(pl.multiple_of(n * (width // 4), width // 4), width // 4)

    @pl.loop(0, 4)
    def _(n):
        cols = tile_of(n)
        for part in range(2):
            one = jnp.dot(state[part], hot[0, :, cols], preferred_element_type=F32)
            two = jnp.dot(state[part], hot[1, :, cols], preferred_element_type=F32)
            product[part, :, cols] = jnp.where(first_side, one, two)

    for part in range(2):
        state[part] = product[part].astype(BF16)

    def layer(g):
        @pl.loop(0, 4)
        def _(n):
            cols = tile_of(n)
            real = gates[g, 0, :, :, :, :, :, :, cols].reshape(width, width // 4)
            imag = gates[g, 1, :, :, :, :, :, :, cols].reshape(width, width // 4)
            real_part, imag_part = complex_dot(state[0], state[1], real, imag)
            product[0, :, cols] = real_part
            product[1, :, cols] = imag_part

    def regroup():
        span = packed * HIGH

        @pl.loop(0, devices // packed)
        def _(a):
            base = pl.multiple_of(a * span, span)
            cols = pl.ds(pl.multiple_of(a * LANES, LANES), LANES)
            for part in range(2):
                for s in range(width // LANES):
                    block = product[part, pl.ds(base, span), s * LANES : (s + 1) * LANES]
                    blocks = [block[i * HIGH : (i + 1) * HIGH] for i in range(packed)]
                    blocks = swap_lane_blocks(blocks, groups)
                    state[part, s * span : (s + 1) * span, cols] = jnp.concatenate(
                        blocks, axis=0
                    ).astype(BF16)

    arrive(0, "q0", "q1")
    send(0, "e0", "e1")
    arrive(0, "c0", "d0", "d1", "e0", "e1")
    layer(0)
    regroup()
    arrive(1, "q0", "q1")
    send(1, "e0", "e1")
    arrive(1, "c0", "d0", "d1", "e0", "e1")
    layer(1)
    for number in range(2, 2 * CYCLES):
        regroup()
        layer(number % 2)

    upper = lax.broadcasted_iota(jnp.int32, (HIGH, width), 0) < share

    @pl.loop(0, devices // 4)
    def _(r):
        base = pl.multiple_of(r * 4 * HIGH, 4 * HIGH)
        to = pl.ds(pl.multiple_of(r * 4 * share, 4 * share), 4 * share)
        for part in range(2):
            slab = product[part, pl.ds(base, 4 * HIGH)]
            lines = [slab[i * HIGH : (i + 1) * HIGH] for i in range(4)]
            lefts, rights = [], []
            for i in range(0, 4, 2):
                lefts.append(jnp.where(upper, lines[i], pltpu.roll(lines[i + 1], share, 0)))
                rights.append(jnp.where(upper, pltpu.roll(lines[i], share, 0), lines[i + 1]))
            left_out[part, to] = jnp.concatenate(lefts, axis=0).astype(BF16)
            right = jnp.concatenate(rights, axis=0).astype(BF16)
            for block in range(width // LANES):
                right_out[part, block // KEPT, block % KEPT, to] = right[
                    :, block * LANES : (block + 1) * LANES
                ]

    lot = left_out.shape[1] // KEPT
    in_pair = quarter * holders
    slot = me % in_pair
    hold = me % holders

    def lot_of(i):
        return pl.ds(pl.multiple_of(i * lot, lot), lot)

    def right_copy(o):
        target = slot ^ o
        return remote(
            right_out.at[:, :, target % holders, lot_of(target // holders)],
            right_in.at[slot],
            right_send.at[o],
            right_recv.at[o],
            me ^ o,
        )

    def right_wait(o):
        return remote(
            right_out.at[:, :, 0, lot_of(0)],
            right_in.at[slot ^ o],
            right_send.at[o],
            right_recv.at[o],
            me ^ o,
        )

    def left_copy(o):
        return remote(
            left_out.at[:, lot_of(hold ^ o)],
            left_in.at[:, hold],
            left_send.at[o],
            left_recv.at[o],
            me ^ o,
        )

    def left_wait(o):
        return remote(
            left_out.at[:, lot_of(0)],
            left_in.at[:, hold ^ o],
            left_send.at[o],
            left_recv.at[o],
            me ^ o,
        )

    def start_right(o, carry):
        right_copy(o).start()
        return carry

    lax.fori_loop(4, in_pair, start_right, 0)
    for o in range(1, holders):
        left_copy(o).start()
    lax.fori_loop(1, 4, start_right, 0)
    own_left = pltpu.make_async_copy(
        left_out.at[:, lot_of(hold)], left_in.at[:, hold], own_sem.at[3]
    )
    own_right = pltpu.make_async_copy(
        right_out.at[:, :, slot % holders, lot_of(slot // holders)], right_in.at[slot], own_sem.at[4]
    )
    own_left.start()
    own_right.start()
    own_left.wait()
    own_right.wait()
    for o in range(1, holders):
        left_wait(o).wait_recv()

    def end_right(o, carry):
        right_wait(o).wait_recv()
        return carry

    lax.fori_loop(1, in_pair, end_right, 0)
    arrived = right_in[...]
    both = jnp.concatenate(
        [arrived[:, part].reshape(width, LANES) for part in range(2)], axis=1
    )
    both = jnp.dot(mixer[...], both, preferred_element_type=F32).astype(BF16)
    by_real = jnp.dot(
        left_in[0].reshape(KEPT * lot, width), both, preferred_element_type=F32
    )
    by_imag = jnp.dot(
        left_in[1].reshape(KEPT * lot, width), both, preferred_element_type=F32
    )
    partial = jnp.concatenate(
        [
            by_real[:, :LANES] - by_imag[:, LANES:],
            by_real[:, LANES:] + by_imag[:, :LANES],
        ],
        axis=1,
    )
    top = lax.broadcasted_iota(jnp.int32, (HIGH, 2 * LANES), 0) < share
    for m in range(0, lot // share, 2):
        lines = [partial[h * lot + m * share : h * lot + m * share + HIGH] for h in range(KEPT)]
        evens, odds = [], []
        for h in range(0, KEPT, 2):
            evens.append(jnp.where(top, lines[h], pltpu.roll(lines[h + 1], share, 0)))
            odds.append(jnp.where(top, pltpu.roll(lines[h], share, 0), lines[h + 1]))
        part_out[m] = jnp.concatenate(evens, axis=0).astype(BF16)
        part_out[m + 1] = jnp.concatenate(odds, axis=0).astype(BF16)

    chunks = part_out.shape[0]
    from_slot = me // holders
    my_group = me // chunks

    def part_copy(m):
        return remote(
            part_out.at[m],
            part_in.at[from_slot],
            part_send.at[m],
            part_recv.at[from_slot],
            hold * chunks + m,
        )

    own_part = pltpu.make_async_copy(
        part_out.at[me % chunks], part_in.at[from_slot], part_recv.at[from_slot]
    )

    def start_part(m, carry):
        target = hold * chunks + m

        @pl.when(target != me)
        def _():
            part_copy(m).start()

        @pl.when(target == me)
        def _():
            own_part.start()

        return carry

    lax.fori_loop(0, chunks, start_part, 0)

    def end_part(i, carry):
        pltpu.make_async_copy(part_out.at[0], part_in.at[i], part_recv.at[i]).wait()
        return carry

    lax.fori_loop(0, chunks, end_part, 0)
    scale = (2.0 * SHARED) ** (-0.5)
    for p in range(2):
        total = part_in[p * quarter].astype(F32)
        for j in range(1, quarter):
            total += part_in[p * quarter + j].astype(F32)
        out[p] = (total * scale).astype(BF16)

    def end_part_send(m, carry):
        @pl.when(hold * chunks + m != me)
        def _():
            part_copy(m).wait_send()

        return carry

    lax.fori_loop(0, chunks, end_part_send, 0)
    for g in range(2):
        for name in names:
            gate_copy(g, name).wait_send()

    def end_deal(o, carry):
        deal_copy(o).wait_send()
        return carry

    lax.fori_loop(1, devices, end_deal, 0)

    def end_right_send(o, carry):
        right_copy(o).wait_send()
        return carry

    lax.fori_loop(1, in_pair, end_right_send, 0)
    for o in range(1, holders):
        left_copy(o).wait_send()


def run_whole(dealt, orders, gate_a, gate_b, devices):
    lines, width = dealt.shape[1:]
    depth = gate_a.shape[1]
    rows = devices * HIGH
    quarter = SHARED // width
    lot = devices * HIGH // 2 // KEPT
    chunks = devices // KEPT
    dma = pltpu.SemaphoreType.DMA
    vmem = pl.BlockSpec(memory_space=pltpu.VMEM)
    return pl.pallas_call(
        lambda *refs: whole_kernel(devices, *refs),
        out_shape=jax.ShapeDtypeStruct((2, lines, 2 * LANES), BF16),
        in_specs=[vmem] * 4,
        out_specs=vmem,
        scratch_shapes=[
            pltpu.VMEM((2, 2, 2, 2, 2, 2, 2, depth, width), BF16),
            pltpu.VMEM((devices, lines, width), BF16),
            pltpu.VMEM((2, rows, width), BF16),
            pltpu.VMEM((2, rows, width), F32),
            pltpu.VMEM((2, width, width), BF16),
            pltpu.VMEM((width, width), BF16),
            pltpu.VMEM((2, rows // 2, width), BF16),
            pltpu.VMEM((2, width // (LANES * KEPT), KEPT, rows // 2, LANES), BF16),
            pltpu.VMEM((2, KEPT, lot, width), BF16),
            pltpu.VMEM((quarter * KEPT, 2, width // (LANES * KEPT), lot, LANES), BF16),
            pltpu.VMEM((chunks, lines, 2 * LANES), BF16),
            pltpu.VMEM((chunks, lines, 2 * LANES), BF16),
            dma((5,)),
            dma((devices,)),
            dma((devices,)),
            dma((2, 11)),
            dma((2, 11)),
            dma((KEPT,)),
            dma((KEPT,)),
            dma((quarter * KEPT,)),
            dma((quarter * KEPT,)),
            dma((chunks,)),
            dma((chunks,)),
        ],
        compiler_params=pltpu.CompilerParams(
            collective_id=0, has_side_effects=True, vmem_limit_bytes=60 * 2**20
        ),
    )(dealt, orders, gate_a, gate_b)


def local(branch_in, column_order, gate_a, gate_b):
    join_scale = (2.0 * SHARED) ** (-0.5)
    devices = lax.axis_size("mode")
    me = lax.axis_index("mode")
    branches, parts, rows, width = branch_in.shape
    quarter = SHARED // width
    holders = devices // (2 * quarter)
    share = rows // (quarter * holders)
    pair = me // (quarter * holders)
    dealt = branch_in.reshape(2, 2, parts, holders, share, quarter, width)
    dealt = dealt.transpose(0, 5, 3, 2, 1, 4, 6).reshape(devices, parts, 2, share, width)
    orders = lax.dynamic_slice_in_dim(column_order, 2 * pair, 2, 0)
    lines = 2 * parts * share
    if lines == 2 * HIGH and holders == KEPT and devices == HIGH * KEPT == width // devices:
        done = run_whole(
            dealt.reshape(devices, lines, width), orders, gate_a, gate_b, devices
        )
        return done.reshape(2, lines, 2, LANES)
    whole_a = lax.all_gather(gate_a, "mode", axis=1, tiled=True)
    whole_b = lax.all_gather(gate_b, "mode", axis=1, tiled=True)
    dealt = lax.all_to_all(dealt, "mode", split_axis=0, concat_axis=0, tiled=True)
    state = dealt.transpose(1, 0, 2, 3, 4)
    state = layers_plain(state, orders, whole_a, whole_b)

    split = holders // KEPT
    piece = width // split
    free = devices * rows * width // (SHARED * KEPT)
    own_group = [
        [start * holders + h for h in range(holders)] for start in range(2 * quarter)
    ]
    pair_group = [
        [start * quarter * holders + d for d in range(quarter * holders)] for start in range(2)
    ]
    left = state[:, :, 0].reshape(parts, KEPT, devices // KEPT, share, split, piece)
    left = left.transpose(1, 4, 0, 2, 3, 5).reshape(
        holders, parts, devices // KEPT, share, piece
    )
    left = lax.all_to_all(
        left, "mode", split_axis=0, concat_axis=0, tiled=True, axis_index_groups=own_group
    )
    left = left.transpose(1, 2, 0, 3, 4).reshape(parts, free, piece)
    right = state[:, :, 1].reshape(parts, quarter, split, devices // (quarter * split), share, width)
    line = rows * width
    step = KEPT * free
    if width % step == 0:
        several = width // step
        right = right.reshape(
            parts, quarter, split, devices // (quarter * split), share, several, KEPT, free
        )
        right = right.transpose(1, 6, 2, 0, 3, 4, 5, 7)
        right = right.reshape(
            quarter * KEPT * split, parts, devices // (quarter * split), share, several, free
        )
        right = lax.all_to_all(
            right, "mode", split_axis=0, concat_axis=0, tiled=True, axis_index_groups=pair_group
        )
        right = right.reshape(
            quarter, holders, parts, devices // (quarter * split), share, several, free
        )
        right = right.transpose(2, 3, 1, 4, 0, 5, 6).reshape(parts, piece, free)
    else:
        spans = step // width
        kept_row = KEPT // spans
        right = right.reshape(
            parts, quarter, split, devices // (quarter * split), share, kept_row, free
        )
        own_j = me // holders % quarter
        g_high = own_j % spans
        slots = jnp.zeros(
            (quarter, spans, kept_row, split, parts, devices // (quarter * split), share, free), BF16
        )
        filled = right.transpose(1, 5, 2, 0, 3, 4, 6)
        slots = lax.dynamic_update_slice_in_dim(slots, filled[:, None], g_high, 1)
        slots = slots.reshape(
            quarter * KEPT * split, parts, devices // (quarter * split), share, free
        )
        slots = lax.all_to_all(
            slots, "mode", split_axis=0, concat_axis=0, tiled=True, axis_index_groups=pair_group
        )
        slots = slots.reshape(
            quarter // spans, spans, holders, parts, devices // (quarter * split), share, free
        )
        my_g = me % holders // split
        slots = lax.dynamic_index_in_dim(slots, my_g // kept_row, 1, keepdims=False)
        right = slots.transpose(2, 3, 1, 4, 0, 5).reshape(parts, piece, free)
    real_part, imag_part = complex_dot(left[0], left[1], right[0], right[1])
    partial = jnp.stack([real_part, imag_part], axis=1)
    return finish(partial, join_scale, devices, quarter, split)


def finish(partial, join_scale, devices, quarter, split):
    me = lax.axis_index("mode")
    free = partial.shape[0]
    holders = devices // (2 * quarter)
    sum_group = [
        [((p * quarter + j) * KEPT + g) * split + w for j in range(quarter) for w in range(split)]
        for p in range(2)
        for g in range(KEPT)
    ]
    count = quarter * split
    chunks = partial.astype(BF16).reshape(count, free // count, 2, free)
    chunks = lax.all_to_all(
        chunks, "mode", split_axis=0, concat_axis=0, tiled=True, axis_index_groups=sum_group
    )
    done = (jnp.sum(chunks.astype(F32), axis=0) * join_scale).astype(BF16)
    halves = done.reshape(2, free // (2 * count), 2, free)
    pair = me // (quarter * holders)
    same = lax.dynamic_index_in_dim(halves, pair, 0, keepdims=False)
    other = lax.dynamic_index_in_dim(halves, 1 - pair, 0, keepdims=False)
    same_pairs, other_pairs = [], []
    for d in range(devices):
        p, j, g, w = (
            d // (quarter * holders),
            d // holders % quarter,
            d // split % KEPT,
            d % split,
        )
        base = g * (devices // KEPT) + 2 * (j * split + w)
        same_pairs.append((d, base + p))
        other_pairs.append((d, base + 1 - p))
    from_same = lax.ppermute(same, "mode", same_pairs)
    from_other = lax.ppermute(other, "mode", other_pairs)
    parity = me % 2
    first = jnp.where(parity == 0, from_same, from_other)
    second = jnp.where(parity == 0, from_other, from_same)
    return jnp.stack([first, second])


def solution(mesh):
    in_specs = (
        P(None, None, ("cuts", "mode"), None),
        P(),
        P(None, "mode", None),
        P(None, "mode", None),
    )
    out_specs = P(None, ("cuts", "mode"), None, None)
    return jax.shard_map(local, mesh=mesh, in_specs=in_specs, out_specs=out_specs, check_vma=False)
```

```python
import jax
import jax.numpy as jnp
from jax import lax
from jax.experimental import pallas as pl
from jax.experimental.pallas import tpu as pltpu
from jax.sharding import PartitionSpec as P

SHARED = 4096
KEPT = 4
CYCLES = 2
F32 = jnp.float32
BF16 = jnp.bfloat16


def complex_dot(left_real, left_imag, right_real, right_imag):
    real_part = jnp.dot(left_real, right_real, preferred_element_type=F32) - jnp.dot(
        left_imag, right_imag, preferred_element_type=F32
    )
    imag_part = jnp.dot(left_real, right_imag, preferred_element_type=F32) + jnp.dot(
        left_imag, right_real, preferred_element_type=F32
    )
    return real_part, imag_part


def layers_plain(state, orders, whole_a, whole_b):
    parts, devices, sides, share, width = state.shape
    group = width // devices
    iota = lax.broadcasted_iota(jnp.int32, (width, width), 0)
    halves = []
    for side in range(sides):
        one_hot = (iota == orders[side][None, :]).astype(BF16)
        piece = state[:, :, side].reshape(parts * devices * share, width)
        halves.append(
            jnp.dot(piece, one_hot, preferred_element_type=F32)
            .astype(BF16)
            .reshape(parts, devices, share, width)
        )
    state = jnp.stack(halves, axis=2)
    for layer in range(2 * CYCLES):
        if layer > 0:
            pieces = state.reshape(parts, devices, sides, share, devices, group)
            state = pieces.transpose(0, 4, 2, 3, 1, 5)
        flat = state.reshape(parts, devices * sides * share, width)
        gate = whole_a if layer % 2 == 0 else whole_b
        state = jnp.stack(complex_dot(flat[0], flat[1], gate[0], gate[1])).astype(BF16)
    return state.reshape(parts, devices, sides, share, width)


LANES = 128
HIGH = 8


def swap_lane_blocks(blocks, group):
    count = len(blocks)
    lane = lax.broadcasted_iota(jnp.int32, (HIGH, LANES), 1) // group
    bit = count // 2
    while bit:
        low = (lane // bit) % 2 == 0
        new = list(blocks)
        for i in range(count):
            if i & bit == 0:
                first, second = blocks[i], blocks[i | bit]
                new[i] = jnp.where(low, first, pltpu.roll(second, bit * group, 1))
                new[i | bit] = jnp.where(low, pltpu.roll(first, LANES - bit * group, 1), second)
        blocks = new
        bit //= 2
    return blocks


def whole_kernel(
    devices,
    dealt,
    orders,
    gate_a,
    gate_b,
    out,
    gates,
    landed,
    state,
    product,
    hot,
    mixer,
    left_out,
    right_out,
    left_in,
    right_in,
    part_out,
    part_in,
    own_sem,
    deal_send,
    deal_recv,
    gate_send,
    gate_recv,
    line_send,
    line_recv,
    left_send,
    left_recv,
    right_send,
    right_recv,
    part_send,
    part_recv,
):
    me = lax.axis_index("mode")
    width = dealt.shape[2]
    rows = state.shape[1]
    groups = width // devices
    packed = LANES // groups
    holders = KEPT
    quarter = SHARED // width
    share = HIGH // 2
    barrier = pltpu.get_barrier_semaphore()

    def greet(o, carry):
        pl.semaphore_signal(barrier, inc=1, device_id={"mode": me ^ o})
        return carry

    lax.fori_loop(1, devices, greet, 0)

    def remote(src, dst, ssem, rsem, target):
        return pltpu.make_async_remote_copy(
            src_ref=src,
            dst_ref=dst,
            send_sem=ssem,
            recv_sem=rsem,
            device_id={"mode": target},
            device_id_type=pl.DeviceIdType.MESH,
        )

    z, y, x, c = (me // 8, me // 4 % 2, me // 2 % 2, me % 2)
    depth_z = devices // 8
    half = depth_z // 2
    every = slice(None)
    lower, higher = pl.ds(0, half), pl.ds(half, half)
    shards = (gate_a, gate_b)
    own = [
        pltpu.make_async_copy(shards[g], gates.at[g, :, z, y, x, c], own_sem.at[g])
        for g in range(2)
    ]
    own_x = pltpu.make_async_copy(dealt.at[me], landed.at[me], own_sem.at[2])
    for copy in own + [own_x]:
        copy.start()

    swaps = (
        {
            "p0": (0, every, y, x, 4),
            "p1": (1, every, y, x, 2),
            "q0": (0, lower, every, x, 2),
            "q1": (1, lower, y, every, 4),
            "r0": (0, higher, every, x, 2),
            "r1": (1, higher, y, every, 4),
            "c0": (every, every, y, x, 1),
            "d0": (0, every, 1 - y, x, 1),
            "d1": (1, every, y, 1 - x, 1),
            "e0": (0, lower, every, 1 - x, 1),
            "e1": (1, lower, 1 - y, every, 1),
            "f0": (0, higher, every, 1 - x, 1),
            "f1": (1, higher, 1 - y, every, 1),
        },
        {
            "p0": (0, z, y, x, 4),
            "p1": (1, z, y, x, 2),
            "q0": (0, lower, every, x, 2),
            "q1": (1, lower, y, every, 4),
            "r0": (0, higher, every, x, 2),
            "r1": (1, higher, y, every, 4),
            "d0": (0, every, every, x, 1),
            "d1": (1, every, y, every, 1),
            "e0": (0, lower, every, 1 - x, 1),
            "e1": (1, lower, 1 - y, every, 1),
            "f0": (0, higher, every, 1 - x, 1),
            "f1": (1, higher, 1 - y, every, 1),
        },
    )

    def swap_copy(g, name):
        part, at_z, at_y, at_x, bit = swaps[g][name]
        k = list(swaps[g]).index(name)
        here = gates.at[g, part, at_z, at_y, at_x, c]
        src = shards[1].at[part] if g == 1 and name in ("p0", "p1") else here
        return remote(src, here, gate_send.at[g, k], gate_recv.at[g, k], me ^ bit)

    def send(g, *which):
        for name in which:
            swap_copy(g, name).start()

    def arrive(g, *which):
        for name in which:
            swap_copy(g, name).wait_recv()

    threads = ((0, every, y, x), (1, 0, every, x), (1, 1, y, every))

    def line_copy(t, up, k):
        g, part, at_y, at_x = threads[t]
        block = z - k if up else z + k
        here = gates.at[g, part, block, at_y, at_x, c]
        src = shards[0] if t == 0 and k == 0 else here
        n = (t * 2 + up) * (depth_z - 1) + k
        return remote(
            src, here, line_send.at[n], line_recv.at[n], me + 8 if up else me - 8
        )

    def line_sends(up, k):
        return (z >= k) & (z < depth_z - 1) if up else (z + k < depth_z) & (z > 0)

    def line_gets(up, k):
        return z >= k + 1 if up else z + 1 + k < depth_z

    def line_start(k, *which):
        for up in (1, 0):

            @pl.when(line_sends(up, k))
            def _():
                for t in which:
                    line_copy(t, up, k).start()

    def line_arrive(k, *which):
        for up in (1, 0):

            @pl.when(line_gets(up, k))
            def _():
                for t in which:
                    g, part, at_y, at_x = threads[t]
                    block = z - 1 - k if up else z + 1 + k
                    here = gates.at[g, part, block, at_y, at_x, c]
                    n = (t * 2 + up) * (depth_z - 1) + k
                    remote(
                        here, here, line_send.at[n], line_recv.at[n], me ^ 8
                    ).wait_recv()

    def line_end():
        for t in range(len(threads)):
            for up in (1, 0):
                for k in range(depth_z - 1):

                    @pl.when(line_sends(up, k))
                    def _():
                        line_copy(t, up, k).wait_send()

    def deal_copy(o):
        return remote(dealt.at[me ^ o], landed.at[me], deal_send.at[o], deal_recv.at[o], me ^ o)

    def start_deal(o, carry):
        deal_copy(o).start()
        return carry

    pl.semaphore_wait(barrier, devices - 1)
    line_start(0, 0)
    send(1, "p0", "p1")
    lax.fori_loop(1, 8, start_deal, 0)
    for copy in own:
        copy.wait()
    line_arrive(0, 0)
    line_start(1, 0)
    arrive(1, "p0", "p1")
    line_start(0, 1, 2)
    line_arrive(1, 0)
    line_start(2, 0)
    lax.fori_loop(8, 16, start_deal, 0)
    line_arrive(2, 0)
    send(0, "p0", "p1", "c0")
    line_arrive(0, 1, 2)
    line_start(1, 1, 2)
    lax.fori_loop(16, 24, start_deal, 0)
    arrive(0, "p0", "p1")
    send(0, "q0", "q1", "r0", "r1", "d0", "d1")
    line_arrive(1, 1, 2)
    line_start(2, 1, 2)
    lax.fori_loop(24, devices, start_deal, 0)
    k = lax.broadcasted_iota(jnp.int32, (1, width), 1)
    natural = (
        (k % 32 // share) * 128 + (k // 64 % 4) * 32 + (k % share) * 8 + (k // 256) * 2 + k // 32 % 2
    )
    mixer[...] = jnp.where(
        lax.broadcasted_iota(jnp.int32, (width, width), 0) == natural, 1.0, 0.0
    ).astype(BF16)
    for side in range(2):
        source = lax.broadcasted_iota(jnp.int32, (width, width), 0)
        hot[side] = jnp.where(source == orders[side : side + 1, :], 1.0, 0.0).astype(BF16)
    arrive(0, "q0", "q1")
    send(0, "e0", "e1")
    line_arrive(2, 1, 2)
    send(1, "q0", "q1", "r0", "r1", "d0", "d1")
    arrive(0, "r0", "r1")
    send(0, "f0", "f1")

    own_x.wait()

    def wait_deal(o, carry):
        remote(dealt.at[me], landed.at[me ^ o], deal_send.at[o], deal_recv.at[o], me ^ o).wait_recv()
        return carry

    lax.fori_loop(1, devices, wait_deal, 0)
    wide = landed[...].astype(F32)
    for part in range(2):
        state[part] = wide[:, part * HIGH : (part + 1) * HIGH].reshape(rows, width).astype(BF16)
    first_side = lax.broadcasted_iota(jnp.int32, (rows, width // 4), 0) % HIGH < share

    def tile_of(n):
        return pl.ds(pl.multiple_of(n * (width // 4), width // 4), width // 4)

    @pl.loop(0, 4)
    def _(n):
        cols = tile_of(n)
        for part in range(2):
            one = jnp.dot(state[part], hot[0, :, cols], preferred_element_type=F32)
            two = jnp.dot(state[part], hot[1, :, cols], preferred_element_type=F32)
            product[part, :, cols] = jnp.where(first_side, one, two)

    for part in range(2):
        state[part] = product[part].astype(BF16)

    def layer(g):
        @pl.loop(0, 4)
        def _(n):
            cols = tile_of(n)
            real = gates[g, 0, :, :, :, :, :, cols].reshape(width, width // 4)
            imag = gates[g, 1, :, :, :, :, :, cols].reshape(width, width // 4)
            real_part, imag_part = complex_dot(state[0], state[1], real, imag)
            product[0, :, cols] = real_part
            product[1, :, cols] = imag_part

    def regroup():
        span = packed * HIGH

        @pl.loop(0, devices // packed)
        def _(a):
            base = pl.multiple_of(a * span, span)
            cols = pl.ds(pl.multiple_of(a * LANES, LANES), LANES)
            for part in range(2):
                for s in range(width // LANES):
                    block = product[part, pl.ds(base, span), s * LANES : (s + 1) * LANES]
                    blocks = [block[i * HIGH : (i + 1) * HIGH] for i in range(packed)]
                    blocks = swap_lane_blocks(blocks, groups)
                    state[part, s * span : (s + 1) * span, cols] = jnp.concatenate(
                        blocks, axis=0
                    ).astype(BF16)

    arrive(0, "c0", "d0", "d1", "e0", "e1", "f0", "f1")
    layer(0)
    regroup()
    arrive(1, "q0", "q1")
    send(1, "e0", "e1")
    arrive(1, "r0", "r1")
    send(1, "f0", "f1")
    arrive(1, "d0", "d1", "e0", "e1", "f0", "f1")
    layer(1)
    for number in range(2, 2 * CYCLES):
        regroup()
        layer(number % 2)

    upper = lax.broadcasted_iota(jnp.int32, (HIGH, width), 0) < share

    @pl.loop(0, devices // 4)
    def _(r):
        base = pl.multiple_of(r * 4 * HIGH, 4 * HIGH)
        to = pl.ds(pl.multiple_of(r * 4 * share, 4 * share), 4 * share)
        for part in range(2):
            slab = product[part, pl.ds(base, 4 * HIGH)]
            lines = [slab[i * HIGH : (i + 1) * HIGH] for i in range(4)]
            lefts, rights = [], []
            for i in range(0, 4, 2):
                lefts.append(jnp.where(upper, lines[i], pltpu.roll(lines[i + 1], share, 0)))
                rights.append(jnp.where(upper, pltpu.roll(lines[i], share, 0), lines[i + 1]))
            left_out[part, to] = jnp.concatenate(lefts, axis=0).astype(BF16)
            right = jnp.concatenate(rights, axis=0).astype(BF16)
            for block in range(width // LANES):
                right_out[part, block // KEPT, block % KEPT, to] = right[
                    :, block * LANES : (block + 1) * LANES
                ]

    lot = left_out.shape[1] // KEPT
    in_pair = quarter * holders
    slot = me % in_pair
    hold = me % holders

    def lot_of(i):
        return pl.ds(pl.multiple_of(i * lot, lot), lot)

    def right_copy(o):
        target = slot ^ o
        return remote(
            right_out.at[:, :, target % holders, lot_of(target // holders)],
            right_in.at[slot],
            right_send.at[o],
            right_recv.at[o],
            me ^ o,
        )

    def right_wait(o):
        return remote(
            right_out.at[:, :, 0, lot_of(0)],
            right_in.at[slot ^ o],
            right_send.at[o],
            right_recv.at[o],
            me ^ o,
        )

    def left_copy(o):
        return remote(
            left_out.at[:, lot_of(hold ^ o)],
            left_in.at[:, hold],
            left_send.at[o],
            left_recv.at[o],
            me ^ o,
        )

    def left_wait(o):
        return remote(
            left_out.at[:, lot_of(0)],
            left_in.at[:, hold ^ o],
            left_send.at[o],
            left_recv.at[o],
            me ^ o,
        )

    def start_right(o, carry):
        right_copy(o).start()
        return carry

    lax.fori_loop(4, in_pair, start_right, 0)
    for o in range(1, holders):
        left_copy(o).start()
    lax.fori_loop(1, 4, start_right, 0)
    own_left = pltpu.make_async_copy(
        left_out.at[:, lot_of(hold)], left_in.at[:, hold], own_sem.at[3]
    )
    own_right = pltpu.make_async_copy(
        right_out.at[:, :, slot % holders, lot_of(slot // holders)], right_in.at[slot], own_sem.at[4]
    )
    own_left.start()
    own_right.start()
    own_left.wait()
    own_right.wait()
    for o in range(1, holders):
        left_wait(o).wait_recv()

    def end_right(o, carry):
        right_wait(o).wait_recv()
        return carry

    lax.fori_loop(1, in_pair, end_right, 0)
    arrived = right_in[...]
    both = jnp.concatenate(
        [arrived[:, part].reshape(width, LANES) for part in range(2)], axis=1
    )
    both = jnp.dot(mixer[...], both, preferred_element_type=F32).astype(BF16)
    by_real = jnp.dot(
        left_in[0].reshape(KEPT * lot, width), both, preferred_element_type=F32
    )
    by_imag = jnp.dot(
        left_in[1].reshape(KEPT * lot, width), both, preferred_element_type=F32
    )
    partial = jnp.concatenate(
        [
            by_real[:, :LANES] - by_imag[:, LANES:],
            by_real[:, LANES:] + by_imag[:, :LANES],
        ],
        axis=1,
    )
    top = lax.broadcasted_iota(jnp.int32, (HIGH, 2 * LANES), 0) < share
    for m in range(0, lot // share, 2):
        lines = [partial[h * lot + m * share : h * lot + m * share + HIGH] for h in range(KEPT)]
        evens, odds = [], []
        for h in range(0, KEPT, 2):
            evens.append(jnp.where(top, lines[h], pltpu.roll(lines[h + 1], share, 0)))
            odds.append(jnp.where(top, pltpu.roll(lines[h], share, 0), lines[h + 1]))
        part_out[m] = jnp.concatenate(evens, axis=0).astype(BF16)
        part_out[m + 1] = jnp.concatenate(odds, axis=0).astype(BF16)

    chunks = part_out.shape[0]
    from_slot = me // holders
    my_group = me // chunks

    def part_copy(m):
        return remote(
            part_out.at[m],
            part_in.at[from_slot],
            part_send.at[m],
            part_recv.at[from_slot],
            hold * chunks + m,
        )

    own_part = pltpu.make_async_copy(
        part_out.at[me % chunks], part_in.at[from_slot], part_recv.at[from_slot]
    )

    def start_part(m, carry):
        target = hold * chunks + m

        @pl.when(target != me)
        def _():
            part_copy(m).start()

        @pl.when(target == me)
        def _():
            own_part.start()

        return carry

    lax.fori_loop(0, chunks, start_part, 0)

    def end_part(i, carry):
        pltpu.make_async_copy(part_out.at[0], part_in.at[i], part_recv.at[i]).wait()
        return carry

    lax.fori_loop(0, chunks, end_part, 0)
    scale = (2.0 * SHARED) ** (-0.5)
    for p in range(2):
        total = part_in[p * quarter].astype(F32)
        for j in range(1, quarter):
            total += part_in[p * quarter + j].astype(F32)
        out[p] = (total * scale).astype(BF16)

    def end_part_send(m, carry):
        @pl.when(hold * chunks + m != me)
        def _():
            part_copy(m).wait_send()

        return carry

    lax.fori_loop(0, chunks, end_part_send, 0)
    for g in range(2):
        for name in swaps[g]:
            swap_copy(g, name).wait_send()
    line_end()

    def end_deal(o, carry):
        deal_copy(o).wait_send()
        return carry

    lax.fori_loop(1, devices, end_deal, 0)

    def end_right_send(o, carry):
        right_copy(o).wait_send()
        return carry

    lax.fori_loop(1, in_pair, end_right_send, 0)
    for o in range(1, holders):
        left_copy(o).wait_send()


def run_whole(dealt, orders, gate_a, gate_b, devices):
    lines, width = dealt.shape[1:]
    depth = gate_a.shape[1]
    rows = devices * HIGH
    quarter = SHARED // width
    lot = devices * HIGH // 2 // KEPT
    chunks = devices // KEPT
    dma = pltpu.SemaphoreType.DMA
    vmem = pl.BlockSpec(memory_space=pltpu.VMEM)
    return pl.pallas_call(
        lambda *refs: whole_kernel(devices, *refs),
        out_shape=jax.ShapeDtypeStruct((2, lines, 2 * LANES), BF16),
        in_specs=[vmem] * 4,
        out_specs=vmem,
        scratch_shapes=[
            pltpu.VMEM((2, 2, devices // 8, 2, 2, 2, depth, width), BF16),
            pltpu.VMEM((devices, lines, width), BF16),
            pltpu.VMEM((2, rows, width), BF16),
            pltpu.VMEM((2, rows, width), F32),
            pltpu.VMEM((2, width, width), BF16),
            pltpu.VMEM((width, width), BF16),
            pltpu.VMEM((2, rows // 2, width), BF16),
            pltpu.VMEM((2, width // (LANES * KEPT), KEPT, rows // 2, LANES), BF16),
            pltpu.VMEM((2, KEPT, lot, width), BF16),
            pltpu.VMEM((quarter * KEPT, 2, width // (LANES * KEPT), lot, LANES), BF16),
            pltpu.VMEM((chunks, lines, 2 * LANES), BF16),
            pltpu.VMEM((chunks, lines, 2 * LANES), BF16),
            dma((5,)),
            dma((devices,)),
            dma((devices,)),
            dma((2, 13)),
            dma((2, 13)),
            dma((6 * (devices // 8 - 1),)),
            dma((6 * (devices // 8 - 1),)),
            dma((KEPT,)),
            dma((KEPT,)),
            dma((quarter * KEPT,)),
            dma((quarter * KEPT,)),
            dma((chunks,)),
            dma((chunks,)),
        ],
        compiler_params=pltpu.CompilerParams(
            collective_id=0, has_side_effects=True, vmem_limit_bytes=60 * 2**20
        ),
    )(dealt, orders, gate_a, gate_b)


def local(branch_in, column_order, gate_a, gate_b):
    join_scale = (2.0 * SHARED) ** (-0.5)
    devices = lax.axis_size("mode")
    me = lax.axis_index("mode")
    branches, parts, rows, width = branch_in.shape
    quarter = SHARED // width
    holders = devices // (2 * quarter)
    share = rows // (quarter * holders)
    pair = me // (quarter * holders)
    dealt = branch_in.reshape(2, 2, parts, holders, share, quarter, width)
    dealt = dealt.transpose(0, 5, 3, 2, 1, 4, 6).reshape(devices, parts, 2, share, width)
    orders = lax.dynamic_slice_in_dim(column_order, 2 * pair, 2, 0)
    lines = 2 * parts * share
    if lines == 2 * HIGH and holders == KEPT and devices == HIGH * KEPT == width // devices:
        done = run_whole(
            dealt.reshape(devices, lines, width), orders, gate_a, gate_b, devices
        )
        return done.reshape(2, lines, 2, LANES)
    whole_a = lax.all_gather(gate_a, "mode", axis=1, tiled=True)
    whole_b = lax.all_gather(gate_b, "mode", axis=1, tiled=True)
    dealt = lax.all_to_all(dealt, "mode", split_axis=0, concat_axis=0, tiled=True)
    state = dealt.transpose(1, 0, 2, 3, 4)
    state = layers_plain(state, orders, whole_a, whole_b)

    split = holders // KEPT
    piece = width // split
    free = devices * rows * width // (SHARED * KEPT)
    own_group = [
        [start * holders + h for h in range(holders)] for start in range(2 * quarter)
    ]
    pair_group = [
        [start * quarter * holders + d for d in range(quarter * holders)] for start in range(2)
    ]
    left = state[:, :, 0].reshape(parts, KEPT, devices // KEPT, share, split, piece)
    left = left.transpose(1, 4, 0, 2, 3, 5).reshape(
        holders, parts, devices // KEPT, share, piece
    )
    left = lax.all_to_all(
        left, "mode", split_axis=0, concat_axis=0, tiled=True, axis_index_groups=own_group
    )
    left = left.transpose(1, 2, 0, 3, 4).reshape(parts, free, piece)
    right = state[:, :, 1].reshape(parts, quarter, split, devices // (quarter * split), share, width)
    line = rows * width
    step = KEPT * free
    if width % step == 0:
        several = width // step
        right = right.reshape(
            parts, quarter, split, devices // (quarter * split), share, several, KEPT, free
        )
        right = right.transpose(1, 6, 2, 0, 3, 4, 5, 7)
        right = right.reshape(
            quarter * KEPT * split, parts, devices // (quarter * split), share, several, free
        )
        right = lax.all_to_all(
            right, "mode", split_axis=0, concat_axis=0, tiled=True, axis_index_groups=pair_group
        )
        right = right.reshape(
            quarter, holders, parts, devices // (quarter * split), share, several, free
        )
        right = right.transpose(2, 3, 1, 4, 0, 5, 6).reshape(parts, piece, free)
    else:
        spans = step // width
        kept_row = KEPT // spans
        right = right.reshape(
            parts, quarter, split, devices // (quarter * split), share, kept_row, free
        )
        own_j = me // holders % quarter
        g_high = own_j % spans
        slots = jnp.zeros(
            (quarter, spans, kept_row, split, parts, devices // (quarter * split), share, free), BF16
        )
        filled = right.transpose(1, 5, 2, 0, 3, 4, 6)
        slots = lax.dynamic_update_slice_in_dim(slots, filled[:, None], g_high, 1)
        slots = slots.reshape(
            quarter * KEPT * split, parts, devices // (quarter * split), share, free
        )
        slots = lax.all_to_all(
            slots, "mode", split_axis=0, concat_axis=0, tiled=True, axis_index_groups=pair_group
        )
        slots = slots.reshape(
            quarter // spans, spans, holders, parts, devices // (quarter * split), share, free
        )
        my_g = me % holders // split
        slots = lax.dynamic_index_in_dim(slots, my_g // kept_row, 1, keepdims=False)
        right = slots.transpose(2, 3, 1, 4, 0, 5).reshape(parts, piece, free)
    real_part, imag_part = complex_dot(left[0], left[1], right[0], right[1])
    partial = jnp.stack([real_part, imag_part], axis=1)
    return finish(partial, join_scale, devices, quarter, split)


def finish(partial, join_scale, devices, quarter, split):
    me = lax.axis_index("mode")
    free = partial.shape[0]
    holders = devices // (2 * quarter)
    sum_group = [
        [((p * quarter + j) * KEPT + g) * split + w for j in range(quarter) for w in range(split)]
        for p in range(2)
        for g in range(KEPT)
    ]
    count = quarter * split
    chunks = partial.astype(BF16).reshape(count, free // count, 2, free)
    chunks = lax.all_to_all(
        chunks, "mode", split_axis=0, concat_axis=0, tiled=True, axis_index_groups=sum_group
    )
    done = (jnp.sum(chunks.astype(F32), axis=0) * join_scale).astype(BF16)
    halves = done.reshape(2, free // (2 * count), 2, free)
    pair = me // (quarter * holders)
    same = lax.dynamic_index_in_dim(halves, pair, 0, keepdims=False)
    other = lax.dynamic_index_in_dim(halves, 1 - pair, 0, keepdims=False)
    same_pairs, other_pairs = [], []
    for d in range(devices):
        p, j, g, w = (
            d // (quarter * holders),
            d // holders % quarter,
            d // split % KEPT,
            d % split,
        )
        base = g * (devices // KEPT) + 2 * (j * split + w)
        same_pairs.append((d, base + p))
        other_pairs.append((d, base + 1 - p))
    from_same = lax.ppermute(same, "mode", same_pairs)
    from_other = lax.ppermute(other, "mode", other_pairs)
    parity = me % 2
    first = jnp.where(parity == 0, from_same, from_other)
    second = jnp.where(parity == 0, from_other, from_same)
    return jnp.stack([first, second])


def solution(mesh):
    in_specs = (
        P(None, None, ("cuts", "mode"), None),
        P(),
        P(None, "mode", None),
        P(None, "mode", None),
    )
    out_specs = P(None, ("cuts", "mode"), None, None)
    return jax.shard_map(local, mesh=mesh, in_specs=in_specs, out_specs=out_specs, check_vma=False)
```

```python
import jax
import jax.numpy as jnp
from jax import lax
from jax.experimental import pallas as pl
from jax.experimental.pallas import tpu as pltpu
from jax.sharding import PartitionSpec as P

SHARED = 4096
KEPT = 4
CYCLES = 2
F32 = jnp.float32
BF16 = jnp.bfloat16


def complex_dot(left_real, left_imag, right_real, right_imag):
    real_part = jnp.dot(left_real, right_real, preferred_element_type=F32) - jnp.dot(
        left_imag, right_imag, preferred_element_type=F32
    )
    imag_part = jnp.dot(left_real, right_imag, preferred_element_type=F32) + jnp.dot(
        left_imag, right_real, preferred_element_type=F32
    )
    return real_part, imag_part


def layers_plain(state, orders, whole_a, whole_b):
    parts, devices, sides, share, width = state.shape
    group = width // devices
    iota = lax.broadcasted_iota(jnp.int32, (width, width), 0)
    halves = []
    for side in range(sides):
        one_hot = (iota == orders[side][None, :]).astype(BF16)
        piece = state[:, :, side].reshape(parts * devices * share, width)
        halves.append(
            jnp.dot(piece, one_hot, preferred_element_type=F32)
            .astype(BF16)
            .reshape(parts, devices, share, width)
        )
    state = jnp.stack(halves, axis=2)
    for layer in range(2 * CYCLES):
        if layer > 0:
            pieces = state.reshape(parts, devices, sides, share, devices, group)
            state = pieces.transpose(0, 4, 2, 3, 1, 5)
        flat = state.reshape(parts, devices * sides * share, width)
        gate = whole_a if layer % 2 == 0 else whole_b
        state = jnp.stack(complex_dot(flat[0], flat[1], gate[0], gate[1])).astype(BF16)
    return state.reshape(parts, devices, sides, share, width)


LANES = 128
HIGH = 8


def swap_lane_blocks(blocks, group):
    count = len(blocks)
    lane = lax.broadcasted_iota(jnp.int32, (HIGH, LANES), 1) // group
    bit = count // 2
    while bit:
        low = (lane // bit) % 2 == 0
        new = list(blocks)
        for i in range(count):
            if i & bit == 0:
                first, second = blocks[i], blocks[i | bit]
                new[i] = jnp.where(low, first, pltpu.roll(second, bit * group, 1))
                new[i | bit] = jnp.where(low, pltpu.roll(first, LANES - bit * group, 1), second)
        blocks = new
        bit //= 2
    return blocks


def whole_kernel(
    devices,
    dealt,
    orders,
    gate_a,
    gate_b,
    out,
    gates,
    landed,
    state,
    product,
    hot,
    mixer,
    left_out,
    right_out,
    left_in,
    right_in,
    part_out,
    part_in,
    own_sem,
    deal_send,
    deal_recv,
    gate_send,
    gate_recv,
    line_send,
    line_recv,
    left_send,
    left_recv,
    right_send,
    right_recv,
    part_send,
    part_recv,
):
    me = lax.axis_index("mode")
    width = dealt.shape[2]
    rows = state.shape[1]
    groups = width // devices
    packed = LANES // groups
    holders = KEPT
    quarter = SHARED // width
    share = HIGH // 2
    barrier = pltpu.get_barrier_semaphore()

    def greet(o, carry):
        pl.semaphore_signal(barrier, inc=1, device_id={"mode": me ^ o})
        return carry

    lax.fori_loop(1, devices, greet, 0)

    def remote(src, dst, ssem, rsem, target):
        return pltpu.make_async_remote_copy(
            src_ref=src,
            dst_ref=dst,
            send_sem=ssem,
            recv_sem=rsem,
            device_id={"mode": target},
            device_id_type=pl.DeviceIdType.MESH,
        )

    z, y, x, c = (me // 8, me // 4 % 2, me // 2 % 2, me % 2)
    depth_z = devices // 8
    every = slice(None)
    shards = (gate_a, gate_b)
    own = [
        pltpu.make_async_copy(shards[g], gates.at[g, :, z, y, x, c], own_sem.at[g])
        for g in range(2)
    ]
    own_x = pltpu.make_async_copy(dealt.at[me], landed.at[me], own_sem.at[2])
    for copy in own + [own_x]:
        copy.start()

    swaps = (
        {
            "p0": (0, y, x, 4),
            "p1": (1, y, x, 2),
            "q0": (0, every, x, 2),
            "q1": (1, y, every, 4),
            "c0": (every, y, x, 1),
            "d0": (0, 1 - y, x, 1),
            "d1": (1, y, 1 - x, 1),
            "e0": (0, every, 1 - x, 1),
            "e1": (1, 1 - y, every, 1),
        },
        {
            "q0": (0, every, x, 2),
            "q1": (1, y, every, 4),
            "d0": (0, every, x, 1),
            "d1": (1, y, every, 1),
            "e0": (0, every, 1 - x, 1),
            "e1": (1, 1 - y, every, 1),
            "p0": (0, y, x, 4),
            "p1": (1, y, x, 2),
        },
    )

    def swap_copy(g, name, place):
        part, at_y, at_x, bit = swaps[g][name]
        k = list(swaps[g]).index(name)
        here = gates.at[g, part, z + place, at_y, at_x, c]
        first = name in ("p0", "p1", "c0") and place == 0
        src = (shards[g] if name == "c0" else shards[g].at[part]) if first else here
        n = place + depth_z - 1
        return remote(src, here, gate_send.at[g, k, n], gate_recv.at[g, k, n], me ^ bit)

    def on_round(r, action):
        for place in (0,) if r == 0 else (-r, r):
            if place == 0:
                action(place)
            else:

                @pl.when((z + place >= 0) & (z + place < depth_z))
                def _():
                    action(place)

    def send(g, r, *which):
        def action(place):
            for name in which:
                swap_copy(g, name, place).start()

        on_round(r, action)

    def pass_on(g, r, got, which):
        def action(place):
            for name in got:
                swap_copy(g, name, place).wait_recv()
            for name in which:
                swap_copy(g, name, place).start()

        on_round(r, action)

    def swaps_end(g, recv, *which):
        for r in range(depth_z):

            def action(place):
                for name in which:
                    copy = swap_copy(g, name, place)
                    if recv is True:
                        copy.wait_recv()
                    else:
                        copy.wait_send()

            on_round(r, action)

    threads = ((0, every, y, x), (1, 0, every, x), (1, 1, y, every))

    def line_copy(t, up, k):
        g, part, at_y, at_x = threads[t]
        block = z - k if up else z + k
        here = gates.at[g, part, block, at_y, at_x, c]
        src = shards[0] if t == 0 and k == 0 else here
        n = (t * 2 + up) * (depth_z - 1) + k
        return remote(
            src, here, line_send.at[n], line_recv.at[n], me + 8 if up else me - 8
        )

    def line_sends(up, k):
        return (z >= k) & (z < depth_z - 1) if up else (z + k < depth_z) & (z > 0)

    def line_gets(up, k):
        return z >= k + 1 if up else z + 1 + k < depth_z

    def line_start(k, *which):
        for up in (1, 0):

            @pl.when(line_sends(up, k))
            def _():
                for t in which:
                    line_copy(t, up, k).start()

    def line_arrive(k, *which):
        for up in (1, 0):

            @pl.when(line_gets(up, k))
            def _():
                for t in which:
                    g, part, at_y, at_x = threads[t]
                    block = z - 1 - k if up else z + 1 + k
                    here = gates.at[g, part, block, at_y, at_x, c]
                    n = (t * 2 + up) * (depth_z - 1) + k
                    remote(
                        here, here, line_send.at[n], line_recv.at[n], me ^ 8
                    ).wait_recv()

    def line_end():
        for t in range(len(threads)):
            for up in (1, 0):
                for k in range(depth_z - 1):

                    @pl.when(line_sends(up, k))
                    def _():
                        line_copy(t, up, k).wait_send()

    def deal_copy(o):
        return remote(dealt.at[me ^ o], landed.at[me], deal_send.at[o], deal_recv.at[o], me ^ o)

    def start_deal(o, carry):
        deal_copy(o).start()
        return carry

    pl.semaphore_wait(barrier, devices - 1)
    through = ("q0", "q1", "d0", "d1")
    start = ("p0", "p1", "c0")

    def first_a(r):
        line_arrive(r - 1, 0)
        if r < depth_z - 1:
            line_start(r, 0)
        send(0, r, *start)

    def second_a(r):
        pass_on(0, r, ("p0", "p1"), through)

    def third(g, r):
        pass_on(g, r, ("q0", "q1"), ("e0", "e1"))

    def first_b(r):
        line_arrive(r - 1, 1, 2)
        if r < depth_z - 1:
            line_start(r, 1, 2)
        send(1, r, *through)

    line_start(0, 0)
    send(1, 0, "p0", "p1")
    send(0, 0, *start)
    for copy in own:
        copy.wait()
    pass_on(1, 0, ("p0", "p1"), ())
    line_start(0, 1, 2)
    first_a(1)
    second_a(0)
    send(1, 0, *through)
    lax.fori_loop(1, 12, start_deal, 0)
    first_a(2)
    first_b(1)
    second_a(1)
    lax.fori_loop(12, 20, start_deal, 0)
    first_a(3)
    third(0, 0)
    second_a(2)
    first_b(2)
    lax.fori_loop(20, devices, start_deal, 0)
    third(1, 0)
    third(0, 1)
    second_a(3)
    first_b(3)
    third(1, 1)
    third(0, 2)
    k = lax.broadcasted_iota(jnp.int32, (1, width), 1)
    natural = (
        (k % 32 // share) * 128 + (k // 64 % 4) * 32 + (k % share) * 8 + (k // 256) * 2 + k // 32 % 2
    )
    mixer[...] = jnp.where(
        lax.broadcasted_iota(jnp.int32, (width, width), 0) == natural, 1.0, 0.0
    ).astype(BF16)
    for side in range(2):
        source = lax.broadcasted_iota(jnp.int32, (width, width), 0)
        hot[side] = jnp.where(source == orders[side : side + 1, :], 1.0, 0.0).astype(BF16)
    third(0, 3)
    third(1, 2)
    own_x.wait()

    def wait_deal(o, carry):
        remote(dealt.at[me], landed.at[me ^ o], deal_send.at[o], deal_recv.at[o], me ^ o).wait_recv()
        return carry

    lax.fori_loop(1, devices, wait_deal, 0)
    wide = landed[...].astype(F32)
    for part in range(2):
        state[part] = wide[:, part * HIGH : (part + 1) * HIGH].reshape(rows, width).astype(BF16)
    first_side = lax.broadcasted_iota(jnp.int32, (rows, width // 4), 0) % HIGH < share

    def tile_of(n):
        return pl.ds(pl.multiple_of(n * (width // 4), width // 4), width // 4)

    @pl.loop(0, 4)
    def _(n):
        cols = tile_of(n)
        for part in range(2):
            one = jnp.dot(state[part], hot[0, :, cols], preferred_element_type=F32)
            two = jnp.dot(state[part], hot[1, :, cols], preferred_element_type=F32)
            product[part, :, cols] = jnp.where(first_side, one, two)

    for part in range(2):
        state[part] = product[part].astype(BF16)

    def layer(g):
        @pl.loop(0, 4)
        def _(n):
            cols = tile_of(n)
            real = gates[g, 0, :, :, :, :, :, cols].reshape(width, width // 4)
            imag = gates[g, 1, :, :, :, :, :, cols].reshape(width, width // 4)
            real_part, imag_part = complex_dot(state[0], state[1], real, imag)
            product[0, :, cols] = real_part
            product[1, :, cols] = imag_part

    def regroup():
        span = packed * HIGH

        @pl.loop(0, devices // packed)
        def _(a):
            base = pl.multiple_of(a * span, span)
            cols = pl.ds(pl.multiple_of(a * LANES, LANES), LANES)
            for part in range(2):
                for s in range(width // LANES):
                    block = product[part, pl.ds(base, span), s * LANES : (s + 1) * LANES]
                    blocks = [block[i * HIGH : (i + 1) * HIGH] for i in range(packed)]
                    blocks = swap_lane_blocks(blocks, groups)
                    state[part, s * span : (s + 1) * span, cols] = jnp.concatenate(
                        blocks, axis=0
                    ).astype(BF16)

    swaps_end(0, True, "c0", "d0", "d1", "e0", "e1")
    layer(0)
    regroup()
    third(1, 3)
    swaps_end(1, True, "d0", "d1", "e0", "e1")
    layer(1)
    for number in range(2, 2 * CYCLES):
        regroup()
        layer(number % 2)

    upper = lax.broadcasted_iota(jnp.int32, (HIGH, width), 0) < share

    @pl.loop(0, devices // 4)
    def _(r):
        base = pl.multiple_of(r * 4 * HIGH, 4 * HIGH)
        to = pl.ds(pl.multiple_of(r * 4 * share, 4 * share), 4 * share)
        for part in range(2):
            slab = product[part, pl.ds(base, 4 * HIGH)]
            lines = [slab[i * HIGH : (i + 1) * HIGH] for i in range(4)]
            lefts, rights = [], []
            for i in range(0, 4, 2):
                lefts.append(jnp.where(upper, lines[i], pltpu.roll(lines[i + 1], share, 0)))
                rights.append(jnp.where(upper, pltpu.roll(lines[i], share, 0), lines[i + 1]))
            left_out[part, to] = jnp.concatenate(lefts, axis=0).astype(BF16)
            right = jnp.concatenate(rights, axis=0).astype(BF16)
            for block in range(width // LANES):
                right_out[part, block // KEPT, block % KEPT, to] = right[
                    :, block * LANES : (block + 1) * LANES
                ]

    lot = left_out.shape[1] // KEPT
    in_pair = quarter * holders
    slot = me % in_pair
    hold = me % holders

    def lot_of(i):
        return pl.ds(pl.multiple_of(i * lot, lot), lot)

    def right_copy(o):
        target = slot ^ o
        return remote(
            right_out.at[:, :, target % holders, lot_of(target // holders)],
            right_in.at[slot],
            right_send.at[o],
            right_recv.at[o],
            me ^ o,
        )

    def right_wait(o):
        return remote(
            right_out.at[:, :, 0, lot_of(0)],
            right_in.at[slot ^ o],
            right_send.at[o],
            right_recv.at[o],
            me ^ o,
        )

    def left_copy(o):
        return remote(
            left_out.at[:, lot_of(hold ^ o)],
            left_in.at[:, hold],
            left_send.at[o],
            left_recv.at[o],
            me ^ o,
        )

    def left_wait(o):
        return remote(
            left_out.at[:, lot_of(0)],
            left_in.at[:, hold ^ o],
            left_send.at[o],
            left_recv.at[o],
            me ^ o,
        )

    def start_right(o, carry):
        right_copy(o).start()
        return carry

    lax.fori_loop(4, in_pair, start_right, 0)
    for o in range(1, holders):
        left_copy(o).start()
    lax.fori_loop(1, 4, start_right, 0)
    own_left = pltpu.make_async_copy(
        left_out.at[:, lot_of(hold)], left_in.at[:, hold], own_sem.at[3]
    )
    own_right = pltpu.make_async_copy(
        right_out.at[:, :, slot % holders, lot_of(slot // holders)], right_in.at[slot], own_sem.at[4]
    )
    own_left.start()
    own_right.start()
    own_left.wait()
    own_right.wait()
    for o in range(1, holders):
        left_wait(o).wait_recv()

    def end_right(o, carry):
        right_wait(o).wait_recv()
        return carry

    lax.fori_loop(1, in_pair, end_right, 0)
    arrived = right_in[...]
    both = jnp.concatenate(
        [arrived[:, part].reshape(width, LANES) for part in range(2)], axis=1
    )
    both = jnp.dot(mixer[...], both, preferred_element_type=F32).astype(BF16)
    by_real = jnp.dot(
        left_in[0].reshape(KEPT * lot, width), both, preferred_element_type=F32
    )
    by_imag = jnp.dot(
        left_in[1].reshape(KEPT * lot, width), both, preferred_element_type=F32
    )
    partial = jnp.concatenate(
        [
            by_real[:, :LANES] - by_imag[:, LANES:],
            by_real[:, LANES:] + by_imag[:, :LANES],
        ],
        axis=1,
    )
    top = lax.broadcasted_iota(jnp.int32, (HIGH, 2 * LANES), 0) < share
    for m in range(0, lot // share, 2):
        lines = [partial[h * lot + m * share : h * lot + m * share + HIGH] for h in range(KEPT)]
        evens, odds = [], []
        for h in range(0, KEPT, 2):
            evens.append(jnp.where(top, lines[h], pltpu.roll(lines[h + 1], share, 0)))
            odds.append(jnp.where(top, pltpu.roll(lines[h], share, 0), lines[h + 1]))
        part_out[m] = jnp.concatenate(evens, axis=0).astype(BF16)
        part_out[m + 1] = jnp.concatenate(odds, axis=0).astype(BF16)

    chunks = part_out.shape[0]
    from_slot = me // holders
    my_group = me // chunks

    def part_copy(m):
        return remote(
            part_out.at[m],
            part_in.at[from_slot],
            part_send.at[m],
            part_recv.at[from_slot],
            hold * chunks + m,
        )

    own_part = pltpu.make_async_copy(
        part_out.at[me % chunks], part_in.at[from_slot], part_recv.at[from_slot]
    )

    def start_part(m, carry):
        target = hold * chunks + m

        @pl.when(target != me)
        def _():
            part_copy(m).start()

        @pl.when(target == me)
        def _():
            own_part.start()

        return carry

    lax.fori_loop(0, chunks, start_part, 0)

    def end_part(i, carry):
        pltpu.make_async_copy(part_out.at[0], part_in.at[i], part_recv.at[i]).wait()
        return carry

    lax.fori_loop(0, chunks, end_part, 0)
    scale = (2.0 * SHARED) ** (-0.5)
    for p in range(2):
        total = part_in[p * quarter].astype(F32)
        for j in range(1, quarter):
            total += part_in[p * quarter + j].astype(F32)
        out[p] = (total * scale).astype(BF16)

    def end_part_send(m, carry):
        @pl.when(hold * chunks + m != me)
        def _():
            part_copy(m).wait_send()

        return carry

    lax.fori_loop(0, chunks, end_part_send, 0)
    swaps_end(0, False, *swaps[0])
    swaps_end(1, False, *list(swaps[1])[:6])
    for name in ("p0", "p1"):
        swap_copy(1, name, 0).wait_send()
    line_end()

    def end_deal(o, carry):
        deal_copy(o).wait_send()
        return carry

    lax.fori_loop(1, devices, end_deal, 0)

    def end_right_send(o, carry):
        right_copy(o).wait_send()
        return carry

    lax.fori_loop(1, in_pair, end_right_send, 0)
    for o in range(1, holders):
        left_copy(o).wait_send()


def run_whole(dealt, orders, gate_a, gate_b, devices):
    lines, width = dealt.shape[1:]
    depth = gate_a.shape[1]
    rows = devices * HIGH
    quarter = SHARED // width
    lot = devices * HIGH // 2 // KEPT
    chunks = devices // KEPT
    dma = pltpu.SemaphoreType.DMA
    vmem = pl.BlockSpec(memory_space=pltpu.VMEM)
    return pl.pallas_call(
        lambda *refs: whole_kernel(devices, *refs),
        out_shape=jax.ShapeDtypeStruct((2, lines, 2 * LANES), BF16),
        in_specs=[vmem] * 4,
        out_specs=vmem,
        scratch_shapes=[
            pltpu.VMEM((2, 2, devices // 8, 2, 2, 2, depth, width), BF16),
            pltpu.VMEM((devices, lines, width), BF16),
            pltpu.VMEM((2, rows, width), BF16),
            pltpu.VMEM((2, rows, width), F32),
            pltpu.VMEM((2, width, width), BF16),
            pltpu.VMEM((width, width), BF16),
            pltpu.VMEM((2, rows // 2, width), BF16),
            pltpu.VMEM((2, width // (LANES * KEPT), KEPT, rows // 2, LANES), BF16),
            pltpu.VMEM((2, KEPT, lot, width), BF16),
            pltpu.VMEM((quarter * KEPT, 2, width // (LANES * KEPT), lot, LANES), BF16),
            pltpu.VMEM((chunks, lines, 2 * LANES), BF16),
            pltpu.VMEM((chunks, lines, 2 * LANES), BF16),
            dma((5,)),
            dma((devices,)),
            dma((devices,)),
            dma((2, 9, 2 * (devices // 8) - 1)),
            dma((2, 9, 2 * (devices // 8) - 1)),
            dma((6 * (devices // 8 - 1),)),
            dma((6 * (devices // 8 - 1),)),
            dma((KEPT,)),
            dma((KEPT,)),
            dma((quarter * KEPT,)),
            dma((quarter * KEPT,)),
            dma((chunks,)),
            dma((chunks,)),
        ],
        compiler_params=pltpu.CompilerParams(
            collective_id=0, has_side_effects=True, vmem_limit_bytes=60 * 2**20
        ),
    )(dealt, orders, gate_a, gate_b)


def local(branch_in, column_order, gate_a, gate_b):
    join_scale = (2.0 * SHARED) ** (-0.5)
    devices = lax.axis_size("mode")
    me = lax.axis_index("mode")
    branches, parts, rows, width = branch_in.shape
    quarter = SHARED // width
    holders = devices // (2 * quarter)
    share = rows // (quarter * holders)
    pair = me // (quarter * holders)
    dealt = branch_in.reshape(2, 2, parts, holders, share, quarter, width)
    dealt = dealt.transpose(0, 5, 3, 2, 1, 4, 6).reshape(devices, parts, 2, share, width)
    orders = lax.dynamic_slice_in_dim(column_order, 2 * pair, 2, 0)
    lines = 2 * parts * share
    if lines == 2 * HIGH and holders == KEPT and devices == HIGH * KEPT == width // devices:
        done = run_whole(
            dealt.reshape(devices, lines, width), orders, gate_a, gate_b, devices
        )
        return done.reshape(2, lines, 2, LANES)
    whole_a = lax.all_gather(gate_a, "mode", axis=1, tiled=True)
    whole_b = lax.all_gather(gate_b, "mode", axis=1, tiled=True)
    dealt = lax.all_to_all(dealt, "mode", split_axis=0, concat_axis=0, tiled=True)
    state = dealt.transpose(1, 0, 2, 3, 4)
    state = layers_plain(state, orders, whole_a, whole_b)

    split = holders // KEPT
    piece = width // split
    free = devices * rows * width // (SHARED * KEPT)
    own_group = [
        [start * holders + h for h in range(holders)] for start in range(2 * quarter)
    ]
    pair_group = [
        [start * quarter * holders + d for d in range(quarter * holders)] for start in range(2)
    ]
    left = state[:, :, 0].reshape(parts, KEPT, devices // KEPT, share, split, piece)
    left = left.transpose(1, 4, 0, 2, 3, 5).reshape(
        holders, parts, devices // KEPT, share, piece
    )
    left = lax.all_to_all(
        left, "mode", split_axis=0, concat_axis=0, tiled=True, axis_index_groups=own_group
    )
    left = left.transpose(1, 2, 0, 3, 4).reshape(parts, free, piece)
    right = state[:, :, 1].reshape(parts, quarter, split, devices // (quarter * split), share, width)
    line = rows * width
    step = KEPT * free
    if width % step == 0:
        several = width // step
        right = right.reshape(
            parts, quarter, split, devices // (quarter * split), share, several, KEPT, free
        )
        right = right.transpose(1, 6, 2, 0, 3, 4, 5, 7)
        right = right.reshape(
            quarter * KEPT * split, parts, devices // (quarter * split), share, several, free
        )
        right = lax.all_to_all(
            right, "mode", split_axis=0, concat_axis=0, tiled=True, axis_index_groups=pair_group
        )
        right = right.reshape(
            quarter, holders, parts, devices // (quarter * split), share, several, free
        )
        right = right.transpose(2, 3, 1, 4, 0, 5, 6).reshape(parts, piece, free)
    else:
        spans = step // width
        kept_row = KEPT // spans
        right = right.reshape(
            parts, quarter, split, devices // (quarter * split), share, kept_row, free
        )
        own_j = me // holders % quarter
        g_high = own_j % spans
        slots = jnp.zeros(
            (quarter, spans, kept_row, split, parts, devices // (quarter * split), share, free), BF16
        )
        filled = right.transpose(1, 5, 2, 0, 3, 4, 6)
        slots = lax.dynamic_update_slice_in_dim(slots, filled[:, None], g_high, 1)
        slots = slots.reshape(
            quarter * KEPT * split, parts, devices // (quarter * split), share, free
        )
        slots = lax.all_to_all(
            slots, "mode", split_axis=0, concat_axis=0, tiled=True, axis_index_groups=pair_group
        )
        slots = slots.reshape(
            quarter // spans, spans, holders, parts, devices // (quarter * split), share, free
        )
        my_g = me % holders // split
        slots = lax.dynamic_index_in_dim(slots, my_g // kept_row, 1, keepdims=False)
        right = slots.transpose(2, 3, 1, 4, 0, 5).reshape(parts, piece, free)
    real_part, imag_part = complex_dot(left[0], left[1], right[0], right[1])
    partial = jnp.stack([real_part, imag_part], axis=1)
    return finish(partial, join_scale, devices, quarter, split)


def finish(partial, join_scale, devices, quarter, split):
    me = lax.axis_index("mode")
    free = partial.shape[0]
    holders = devices // (2 * quarter)
    sum_group = [
        [((p * quarter + j) * KEPT + g) * split + w for j in range(quarter) for w in range(split)]
        for p in range(2)
        for g in range(KEPT)
    ]
    count = quarter * split
    chunks = partial.astype(BF16).reshape(count, free // count, 2, free)
    chunks = lax.all_to_all(
        chunks, "mode", split_axis=0, concat_axis=0, tiled=True, axis_index_groups=sum_group
    )
    done = (jnp.sum(chunks.astype(F32), axis=0) * join_scale).astype(BF16)
    halves = done.reshape(2, free // (2 * count), 2, free)
    pair = me // (quarter * holders)
    same = lax.dynamic_index_in_dim(halves, pair, 0, keepdims=False)
    other = lax.dynamic_index_in_dim(halves, 1 - pair, 0, keepdims=False)
    same_pairs, other_pairs = [], []
    for d in range(devices):
        p, j, g, w = (
            d // (quarter * holders),
            d // holders % quarter,
            d // split % KEPT,
            d % split,
        )
        base = g * (devices // KEPT) + 2 * (j * split + w)
        same_pairs.append((d, base + p))
        other_pairs.append((d, base + 1 - p))
    from_same = lax.ppermute(same, "mode", same_pairs)
    from_other = lax.ppermute(other, "mode", other_pairs)
    parity = me % 2
    first = jnp.where(parity == 0, from_same, from_other)
    second = jnp.where(parity == 0, from_other, from_same)
    return jnp.stack([first, second])


def solution(mesh):
    in_specs = (
        P(None, None, ("cuts", "mode"), None),
        P(),
        P(None, "mode", None),
        P(None, "mode", None),
    )
    out_specs = P(None, ("cuts", "mode"), None, None)
    return jax.shard_map(local, mesh=mesh, in_specs=in_specs, out_specs=out_specs, check_vma=False)
```
